32 devices in a mesh: rows: 16 (over z, y, x), feat: 2 (over core).
Axes of the slice: x: 2, y: 2, z: 4, core: 2. Of those that a mesh axis runs over, the one named last changes fastest.
Arguments:
- embeddings: bfloat16 [12288, 768], P('rows', 'feat'), may hold values from -6 to 6
- factor: float32 [12288, 256], P(('rows', 'feat')), may hold values from -0.1 to 0.1, as said below
- residual_diag: float32 [12288], P(('rows', 'feat')), may hold values from 0.5 to 1.5
- pivots: int32 [2, 256], replicated, may hold values from 0 to 12287, as said below
Outputs:
- new_columns: float32 [2, 12288, 256], P(None, ('rows', 'feat'))
- residual_out: float32 [12288], P(('rows', 'feat'))
The draws below stay inside these ranges and needn't reach their ends.
Inputs may be any that keep to these rules, and one draw needn't show every extreme that they name: Each block's 256 pivots are distinct and increasing, the two blocks share none, and in each block at most 32 pivots lie among the 768 candidates of one index of rows; some index holds exactly 32 in every block. `factor`: entries are independent.
All inputs are finite; a program needn't handle non-finite values.
Results may differ from the reference program's by a relative error of at most 0.0003.
Values may be sent and summed in bfloat16 or wider, within the bound.
No kernel may reach another device: no remote copies, remote signals or barrier semaphores. Data moves between devices by JAX's collectives and lax.ppermute only.
A program may use at most 64 MiB of HBM per device.

```python
import jax
import jax.numpy as jnp
from jax import lax

D = 768
R = 256
B = 256
ROWS_DEV = 768
NCAND = 12288
CAP = 32
N_ROWS = 16


def draw_factor(key, part):
    factor_key = jax.random.fold_in(key, 29)
    values = 0.03 * jax.random.truncated_normal(factor_key, -3.3, 3.3, (NCAND, R), jnp.float32)
    return values.astype(jnp.float32)


def draw_pivots(key, part):
    slot_count = N_ROWS * CAP
    stripe = ROWS_DEV // (2 * CAP)
    block_list = []
    for block_id in range(2):
        block_key = jax.random.fold_in(key, 11 + block_id)
        score_key, full_key, jitter_key = jax.random.split(block_key, 3)
        scores = jax.random.randint(score_key, (slot_count,), 0, 1 << 18)
        slot_ids = jnp.arange(slot_count, dtype=jnp.int32)
        full_device = jax.random.randint(full_key, (), 0, N_ROWS)
        boosted = scores + jnp.where(slot_ids // CAP == full_device, 1 << 19, 0)
        keyed = boosted * slot_count + slot_ids
        top_values, top_slots = lax.top_k(keyed, B)
        device = top_slots // CAP
        slot_pos = top_slots % CAP
        jitter = jax.random.randint(jitter_key, (B,), 0, stripe)
        chosen = device * ROWS_DEV + (block_id * CAP + slot_pos) * stripe + jitter
        block_list.append(jnp.sort(chosen))
    return jnp.stack(block_list).astype(jnp.int32)


def block_levels(rng, extent, shards, least, top_value):
    def one(axis_at, parts):
        steps = jax.random.uniform(jax.random.fold_in(jax.random.fold_in(rng, 6), axis_at), (parts,), jnp.float32, least / len(shards), top_value / len(shards))
        return jnp.repeat(jnp.exp(steps), extent[axis_at] // parts).reshape((-1,) + (1,) * (len(extent) - axis_at - 1))

    gain = one(*shards[0])
    for cut in shards[1:]:
        gain = gain * one(*cut)
    return gain


def bell_draw(key, shape, width, reach, shards=(), held_as=jnp.bfloat16):
    result = jax.random.normal(key, shape, jnp.float32) * width
    if len(shards) > 0:
        result = block_levels(key, shape, shards, -0.22, 0.18) * result
    return jnp.clip(result, min=-reach, max=reach).astype(held_as)


def setup_inputs(seed: int = 0) -> dict:
    splits = jax.random.split(jax.random.key(seed), 5)
    return {
        "embeddings": bell_draw(splits[0], (NCAND, D), 1.0, 6.0, ((0, 16), (1, 2))),
        "factor": draw_factor(jax.random.fold_in(splits[4], 71), 0),
        "residual_diag": jnp.clip(0.5 + 1.0 * jax.random.uniform(splits[2], (NCAND,), jnp.float32) ** block_levels(splits[2], (NCAND,), ((0, 32),), -0.2, 0.2), 0.5, 1.5),
        "pivots": draw_pivots(jax.random.fold_in(splits[4], 71), 0),
    }


ridge_weight = 2.0

def block_columns(embeddings, row_norms, current, chosen_ids):
    chosen = embeddings[chosen_ids]
    chosen_norms = row_norms[chosen_ids]
    dot_panel = jnp.dot(embeddings.astype(jnp.float32), chosen.T.astype(jnp.float32), preferred_element_type=jnp.float32)
    kernel_panel = jnp.exp(-(row_norms[:, None] + chosen_norms[None, :] - 2.0 * dot_panel) / (2.0 * D))
    row_ids = jnp.arange(embeddings.shape[0], dtype=jnp.int32)
    kernel_panel = kernel_panel + ridge_weight * (row_ids[:, None] == chosen_ids[None, :]).astype(jnp.float32)
    kernel_panel = kernel_panel - jnp.dot(current.astype(jnp.float32), current[chosen_ids].T.astype(jnp.float32), precision=lax.Precision.HIGHEST, preferred_element_type=jnp.float32)
    chol_lower = jnp.linalg.cholesky(kernel_panel[chosen_ids])
    return jax.scipy.linalg.solve_triangular(chol_lower, kernel_panel.T, lower=True).T

def reference(embeddings, factor, residual_diag, pivots):
    wide_rows = embeddings.astype(jnp.float32)
    row_norms = jnp.sum(wide_rows * wide_rows, axis=1)
    current = factor
    fresh_list = []
    for block_id in range(2):
        fresh_cols = block_columns(embeddings, row_norms, current, pivots[block_id].astype(jnp.int32))
        fresh_list.append(fresh_cols)
        current = jnp.concatenate([current, fresh_cols], axis=1)
    removed = jnp.sum(fresh_list[0] * fresh_list[0], axis=1) + jnp.sum(fresh_list[1] * fresh_list[1], axis=1)
    return (jnp.stack(fresh_list), residual_diag - removed)
```

```python
import jax
import jax.numpy as jnp
from jax import lax
from jax.experimental import pallas as pl
from jax.experimental.pallas import tpu as pltpu
from jax.sharding import PartitionSpec as P


ridge_weight = 2.0
slab_rows = 32
group_cols = 16
lanes = 128


def split(values):
    high = values.astype(jnp.bfloat16)
    low = (values - high.astype(jnp.float32)).astype(jnp.bfloat16)
    return high, low


def dot_nt(left, right):
    return lax.dot_general(left, right, (((1,), (1,)), ((), ())), preferred_element_type=jnp.float32)


def dot_tn(left, right):
    return lax.dot_general(left, right, (((0,), (0,)), ((), ())), preferred_element_type=jnp.float32)


def dot_nn(left, right):
    return jnp.dot(left, right, preferred_element_type=jnp.float32)


def stages_of(count):
    found = []
    stride = 1
    while stride < count:
        size = min(4, count // stride)
        found.append((stride, size))
        stride *= size
    return found[::-1]


def column_of(row):
    return jnp.transpose(jnp.broadcast_to(row, (8, row.shape[1])))[:, 0:1]


def pack_body(place, pivots, embeddings, factor, picked_x, picked_f, other_f, other_x, *, capacity):
    local_rows, half_rows = embeddings.shape[0], factor.shape[0]
    width = factor.shape[1] // 2
    block_count, pivot_count = pivots.shape
    feat = place[1]
    rows_start = place[0] * local_rows
    half_start = feat * half_rows
    other_x[...] = embeddings[pl.ds((1 - feat) * half_rows, half_rows), :]
    factor_high, factor_low = split(factor[...])
    slots = lax.broadcasted_iota(jnp.int32, (capacity, 1), 0)

    def one_hot(column, start, count):
        ids = rows_start + start + lax.broadcasted_iota(jnp.int32, (1, count), 1)
        found = jnp.sum((column == ids).astype(jnp.float32), axis=0, keepdims=True)
        before = (column >= rows_start) & (column < ids)
        rank = jnp.sum(before.astype(jnp.float32), axis=0, keepdims=True)
        hits = (rank.astype(jnp.int32) == slots) & (found > 0.5)
        return hits.astype(jnp.float32).astype(jnp.bfloat16)

    for block in range(block_count):
        column = column_of(pivots[block : block + 1, :])
        at = slice(block * capacity, (block + 1) * capacity)
        hot = one_hot(column, 0, local_rows)
        picked_x[at, :] = dot_nn(hot, embeddings[...]).astype(jnp.bfloat16)
        hot = one_hot(column, half_start, half_rows)
        high = dot_nn(hot, factor_high).astype(jnp.bfloat16)
        low = dot_nn(hot, factor_low).astype(jnp.bfloat16)
        first = jnp.concatenate([high[:, :width], low[:, :width]], axis=1)
        second = jnp.concatenate([high[:, width:], low[:, width:]], axis=1)
        picked_f[at, :] = jnp.where(feat == 0, first, second)
        other_f[at, :] = jnp.where(feat == 0, second, first)


def eliminate(work, count, total):
    for start in range(0, count, slab_rows):
        first = start // lanes * lanes
        width = total - first
        reps = width // lanes
        rows = work[start : start + slab_rows, first:]

        def spread(column):
            return jnp.concatenate([column] * reps, axis=1)

        done = []
        tail = rows
        for group in range(0, slab_rows, group_cols):
            height = slab_rows - group
            ids = lax.broadcasted_iota(jnp.int32, (height, 1), 0)
            base = start - first + group
            columns = [
                jnp.broadcast_to(tail[:, base + t : base + t + 1], (height, lanes))
                for t in range(group_cols)
            ]
            for t in range(group_cols):
                inv = lax.rsqrt(columns[t][t : t + 1, :])
                factors = jnp.where(ids > t, columns[t] * (inv * inv), 0.0)
                for later in range(t + 1, group_cols):
                    columns[later] = columns[later] - factors * columns[later][t : t + 1, :]
                tail = tail - spread(factors) * tail[t : t + 1, :]
                tail = tail * spread(jnp.where(ids == t, inv, 1.0))
            done.append(tail[:group_cols])
            tail = tail[group_cols:]
        rows = jnp.concatenate(done, axis=0)
        work[start : start + slab_rows, first:] = rows
        following = start + slab_rows
        if following >= count:
            break
        high, low = split(rows)
        left = jnp.concatenate([high, high, low], axis=0)
        right = jnp.concatenate([high, low, high], axis=0)
        begin = following
        while begin < count:
            base = begin // lanes * lanes
            end = base + lanes
            update = dot_tn(left[:, base - first : end - first], right[:, base - first :])
            work[begin:end, base:] = work[begin:end, base:] - update[begin - base :]
            begin = end


def main_body(place, pivots, embeddings, other_x, factor, residual, *refs, capacity, stages, piece_count):
    mine = refs[:piece_count]
    theirs = refs[piece_count : 2 * piece_count]
    columns_out, residual_out, work = refs[2 * piece_count :]
    local_rows, feat_cols = embeddings.shape
    half_rows, rank = factor.shape
    block_count, pivot_count = pivots.shape
    total_pivots = block_count * pivot_count
    total = total_pivots + half_rows
    rows_count = 1
    for _, size in stages:
        rows_count *= size
    row, feat = place[0], place[1]
    half_start = row * local_rows + feat * half_rows
    split_blocks = capacity % 16 == 0

    ids = [column_of(pivots[b : b + 1, :]) for b in range(block_count)]
    slot_count = rows_count * capacity * (1 if split_blocks else block_count)
    slot_row = lax.broadcasted_iota(jnp.int32, (1, slot_count), 1)
    order = lax.broadcasted_iota(jnp.int32, (pivot_count, 1), 0)

    def slots_of(pieces, block):
        if not split_blocks:
            return jnp.concatenate([p[...] for p in pieces], axis=0)
        step = block_count * capacity
        return jnp.concatenate(
            [
                p[at + block * capacity : at + (block + 1) * capacity, :]
                for p in pieces
                for at in range(0, p.shape[0], step)
            ],
            axis=0,
        )

    half_width = rank // 2
    x_list, high_list, low_list = [], [], []
    for block in range(block_count):
        column = ids[block]
        owner = ((column.astype(jnp.float32) + 0.5) * (1.0 / local_rows)).astype(jnp.int32)
        earlier = (pivots[block : block + 1, :] < owner * local_rows).astype(jnp.float32)
        pivot_rank = order - jnp.sum(earlier, axis=1, keepdims=True).astype(jnp.int32)
        relative = owner ^ row
        chunk = jnp.zeros_like(relative)
        weight = 1
        for stride, size in stages:
            chunk = chunk + ((relative // stride) & (size - 1)) * weight
            weight *= size
        if split_blocks:
            position = chunk * capacity + pivot_rank
        else:
            position = chunk * (block_count * capacity) + block * capacity + pivot_rank
        hot = (slot_row == position).astype(jnp.float32).astype(jnp.bfloat16)
        own = dot_nn(hot, slots_of(mine, block)).astype(jnp.bfloat16)
        far = dot_nn(hot, slots_of(theirs, block)).astype(jnp.bfloat16)
        x_list.append(jnp.concatenate([own[:, :feat_cols], far[:, :feat_cols]], axis=1))
        mid, end = feat_cols + half_width, feat_cols + 2 * half_width
        high_list.append(jnp.concatenate([own[:, feat_cols:mid], far[:, feat_cols:mid]], axis=1))
        low_list.append(jnp.concatenate([own[:, mid:end], far[:, mid:end]], axis=1))

    own_x = jnp.concatenate([embeddings[pl.ds(feat * half_rows, half_rows), :], other_x[...]], axis=1)
    own_f = factor[...]
    swapped = jnp.concatenate([own_f[:, half_width:], own_f[:, :half_width]], axis=1)
    own_high, own_low = split(jnp.where(feat == 0, own_f, swapped))
    all_x = jnp.concatenate(x_list + [own_x], axis=0)
    all_high = jnp.concatenate(high_list + [own_high], axis=0)
    all_low = jnp.concatenate(low_list + [own_low], axis=0)

    wide = all_x.astype(jnp.float32)
    squares = wide * wide
    norm_column = jnp.sum(squares[:total_pivots], axis=1, keepdims=True)
    square_high, square_low = split(squares)
    ones = jnp.ones((8, square_high.shape[1]), jnp.bfloat16)
    norm_row = (dot_nt(ones, square_high) + dot_nt(ones, square_low))[0:1, :]

    own_ids = half_start + lax.broadcasted_iota(jnp.int32, (1, half_rows), 1)
    id_row = jnp.concatenate([pivots[b : b + 1, :] for b in range(block_count)] + [own_ids], axis=1)
    id_column = jnp.concatenate(ids, axis=0)

    dots = dot_nt(all_x[:total_pivots], all_x)
    left = jnp.concatenate([all_high, all_high, all_low], axis=1)[:total_pivots]
    right = jnp.concatenate([all_high, all_low, all_high], axis=1)
    explained = dot_nt(left, right)
    panel = jnp.exp((2.0 * dots - norm_column - norm_row) * (1.0 / (2 * all_x.shape[1])))
    panel = panel + ridge_weight * (id_row == id_column).astype(jnp.float32)
    work[...] = panel - explained

    eliminate(work, total_pivots, total)

    removed = jnp.zeros((1, half_rows), jnp.float32)
    for block in range(block_count):
        fresh = work[block * pivot_count : (block + 1) * pivot_count, total_pivots:]
        removed = removed + jnp.sum(fresh * fresh, axis=0, keepdims=True)
        columns_out[block] = jnp.transpose(fresh)
    residual_out[...] = residual[...] - removed


def shards(embeddings, factor, residual_diag, pivots):
    half_rows, rank = factor.shape
    feat_cols = embeddings.shape[1]
    rows_count = lax.axis_size("rows")
    block_count, pivot_count = pivots.shape
    capacity = max(2, 2 * pivot_count // rows_count)
    slots = block_count * capacity
    stages = stages_of(rows_count)
    place = jnp.stack([lax.axis_index("rows"), lax.axis_index("feat")]).astype(jnp.int32)
    smem = pl.BlockSpec(memory_space=pltpu.SMEM)
    vmem = pl.BlockSpec(memory_space=pltpu.VMEM)

    def cross(values):
        return lax.ppermute(values, "feat", [(0, 1), (1, 0)])

    def reach(values, offset):
        return lax.ppermute(values, "rows", [(i, i ^ offset) for i in range(rows_count)])

    picked_x, picked_f, other_f, other_x = pl.pallas_call(
        lambda *refs: pack_body(*refs, capacity=capacity),
        out_shape=(
            jax.ShapeDtypeStruct((slots, feat_cols), jnp.bfloat16),
            jax.ShapeDtypeStruct((slots, rank), jnp.bfloat16),
            jax.ShapeDtypeStruct((slots, rank), jnp.bfloat16),
            jax.ShapeDtypeStruct((half_rows, feat_cols), jnp.bfloat16),
        ),
        in_specs=[smem, vmem, vmem, vmem],
        out_specs=(vmem, vmem, vmem, vmem),
        name="pack",
    )(place, pivots, embeddings, factor)
    got_f = cross(other_f)
    far_x = cross(other_x)
    held = jnp.concatenate([picked_x, picked_f + got_f], axis=1)
    for stride, size in stages[:-1]:
        held = jnp.concatenate([held] + [reach(held, stride * j) for j in range(1, size)], axis=0)
    stride, size = stages[-1]
    mine = [held] + [reach(held, stride * j) for j in range(1, size)]
    theirs = [cross(piece) for piece in mine]

    total_pivots = block_count * pivot_count
    columns, residual = pl.pallas_call(
        lambda *refs: main_body(*refs, capacity=capacity, stages=stages, piece_count=len(mine)),
        out_shape=(
            jax.ShapeDtypeStruct((block_count, half_rows, pivot_count), jnp.float32),
            jax.ShapeDtypeStruct((1, half_rows), jnp.float32),
        ),
        in_specs=[smem] + [vmem] * (5 + 2 * len(mine)),
        out_specs=(vmem, vmem),
        scratch_shapes=[pltpu.VMEM((total_pivots, total_pivots + half_rows), jnp.float32)],
        name="extend",
    )(place, pivots, embeddings, far_x, factor, residual_diag[None, :], *mine, *theirs)
    return columns, residual[0]


def solution(mesh):
    return jax.shard_map(
        shards,
        mesh=mesh,
        in_specs=(P("rows", "feat"), P(("rows", "feat"), None), P(("rows", "feat")), P()),
        out_specs=(P(None, ("rows", "feat"), None), P(("rows", "feat"))),
        check_vma=False,
    )
```

```python
import jax
import jax.numpy as jnp
from jax import lax
from jax.experimental import pallas as pl
from jax.experimental.pallas import tpu as pltpu
from jax.sharding import PartitionSpec as P


ridge_weight = 2.0
slab_rows = 32
group_cols = 16
lanes = 128
link_scale = 256.0
vmem_limit = 24 << 20


def split(values):
    high = values.astype(jnp.bfloat16)
    low = (values - high.astype(jnp.float32)).astype(jnp.bfloat16)
    return high, low


def dot_nt(left, right):
    return lax.dot_general(left, right, (((1,), (1,)), ((), ())), preferred_element_type=jnp.float32)


def dot_tn(left, right):
    return lax.dot_general(left, right, (((0,), (0,)), ((), ())), preferred_element_type=jnp.float32)


def dot_nn(left, right):
    return jnp.dot(left, right, preferred_element_type=jnp.float32)


def stages_of(count):
    found = []
    stride = 1
    while stride < count:
        size = min(4, count // stride)
        found.append((stride, size))
        stride *= size
    return found[::-1]


def column_of(row):
    return jnp.transpose(jnp.broadcast_to(row, (8, row.shape[1])))[:, 0:1]


def pack_body(pivots, embeddings, factor, picked_x, picked_f, other_f, *, capacity):
    local_rows, half_rows = embeddings.shape[0], factor.shape[0]
    width = factor.shape[1] // 2
    block_count, pivot_count = pivots.shape
    feat = lax.axis_index("feat")
    rows_start = lax.axis_index("rows") * local_rows
    half_start = feat * half_rows
    factor_high, factor_low = split(factor[...] * link_scale)
    slots = lax.broadcasted_iota(jnp.int32, (capacity, 1), 0)

    def one_hot(column, start, count):
        ids = rows_start + start + lax.broadcasted_iota(jnp.int32, (1, count), 1)
        found = jnp.sum((column == ids).astype(jnp.float32), axis=0, keepdims=True)
        before = (column >= rows_start) & (column < ids)
        rank = jnp.sum(before.astype(jnp.float32), axis=0, keepdims=True)
        hits = (rank.astype(jnp.int32) == slots) & (found > 0.5)
        return hits.astype(jnp.float32).astype(jnp.bfloat16)

    for block in range(block_count):
        column = column_of(pivots[block : block + 1, :])
        at = slice(block * capacity, (block + 1) * capacity)
        hot = one_hot(column, 0, local_rows)
        picked_x[at, :] = dot_nn(hot, embeddings[...]).astype(jnp.bfloat16)
        hot = one_hot(column, half_start, half_rows)
        rows = dot_nn(hot, factor_high) + dot_nn(hot, factor_low)
        first, second = rows[:, :width], rows[:, width:]
        picked_f[at, :] = jnp.where(feat == 0, first, second)
        other_f[at, :] = jnp.where(feat == 0, second, first)


def eliminate(work, count, total):
    for start in range(0, count, slab_rows):
        first = start // lanes * lanes
        width = total - first
        reps = width // lanes
        rows = work[start : start + slab_rows, first:]

        def spread(column):
            return jnp.concatenate([column] * reps, axis=1)

        done = []
        tail = rows
        for group in range(0, slab_rows, group_cols):
            height = slab_rows - group
            ids = lax.broadcasted_iota(jnp.int32, (height, 1), 0)
            base = start - first + group
            columns = [
                jnp.broadcast_to(tail[:, base + t : base + t + 1], (height, lanes))
                for t in range(group_cols)
            ]
            for t in range(group_cols):
                inv = lax.rsqrt(columns[t][t : t + 1, :])
                factors = jnp.where(ids > t, columns[t] * (inv * inv), 0.0)
                for later in range(t + 1, group_cols):
                    columns[later] = columns[later] - factors * columns[later][t : t + 1, :]
                tail = tail - spread(factors) * tail[t : t + 1, :]
                tail = tail * spread(jnp.where(ids == t, inv, 1.0))
            done.append(tail[:group_cols])
            tail = tail[group_cols:]
        rows = jnp.concatenate(done, axis=0)
        work[start : start + slab_rows, first:] = rows
        following = start + slab_rows
        if following >= count:
            break
        high, low = split(rows)
        left = jnp.concatenate([high, high, low], axis=0)
        right = jnp.concatenate([high, low, high], axis=0)
        begin = following
        while begin < count:
            base = begin // lanes * lanes
            end = base + lanes
            update = dot_tn(left[:, base - first : end - first], right[:, base - first :])
            work[begin:end, base:] = work[begin:end, base:] - update[begin - base :]
            begin = end


def main_body(pivots, embeddings, other_x, factor, residual, *refs, capacity, stages_x, stages_f):
    count_x, count_f = stages_x[-1][1], stages_f[-1][1]
    mine_x, refs = refs[:count_x], refs[count_x:]
    theirs_x, refs = refs[:count_x], refs[count_x:]
    mine_f, theirs_f, columns_out, residual_out, work = refs
    local_rows, feat_cols = embeddings.shape
    half_rows, rank = factor.shape
    block_count, pivot_count = pivots.shape
    total_pivots = block_count * pivot_count
    total = total_pivots + half_rows
    rows_count = 1
    for _, size in stages_x:
        rows_count *= size
    row, feat = lax.axis_index("rows"), lax.axis_index("feat")
    half_start = row * local_rows + feat * half_rows
    split_blocks = capacity % 16 == 0

    ids = [column_of(pivots[b : b + 1, :]) for b in range(block_count)]
    slot_count = rows_count * capacity * (1 if split_blocks else block_count)
    slot_row = lax.broadcasted_iota(jnp.int32, (1, slot_count), 1)
    order = lax.broadcasted_iota(jnp.int32, (pivot_count, 1), 0)

    def slots_of(pieces, block):
        if not split_blocks:
            return jnp.concatenate([p[...] for p in pieces], axis=0)
        step = block_count * capacity
        return jnp.concatenate(
            [
                p[at + block * capacity : at + (block + 1) * capacity, :]
                for p in pieces
                for at in range(0, p.shape[0], step)
            ],
            axis=0,
        )

    half_width = rank // 2
    x_list, high_list, low_list = [], [], []
    for block in range(block_count):
        column = ids[block]
        owner = ((column.astype(jnp.float32) + 0.5) * (1.0 / local_rows)).astype(jnp.int32)
        earlier = (pivots[block : block + 1, :] < owner * local_rows).astype(jnp.float32)
        pivot_rank = order - jnp.sum(earlier, axis=1, keepdims=True).astype(jnp.int32)
        relative = owner ^ row

        def hot_of(stages):
            chunk = jnp.zeros_like(relative)
            weight = 1
            for stride, size in stages:
                chunk = chunk + ((relative // stride) & (size - 1)) * weight
                weight *= size
            if split_blocks:
                position = chunk * capacity + pivot_rank
            else:
                position = chunk * (block_count * capacity) + block * capacity + pivot_rank
            return (slot_row == position).astype(jnp.float32).astype(jnp.bfloat16)

        hot_x, hot_f = hot_of(stages_x), hot_of(stages_f)
        x_list.append(
            jnp.concatenate(
                [dot_nn(hot_x, slots_of(side, block)).astype(jnp.bfloat16) for side in (mine_x, theirs_x)], axis=1
            )
        )
        for part in (0, 1):
            (high_list, low_list)[part].append(
                jnp.concatenate(
                    [
                        dot_nn(hot_f, split(slots_of([side], block) * (1.0 / link_scale))[part]).astype(jnp.bfloat16)
                        for side in (mine_f, theirs_f)
                    ],
                    axis=1,
                )
            )

    own_at = pl.ds(feat * half_rows, half_rows)
    own_x = jnp.concatenate([embeddings[own_at, :], other_x[own_at, :]], axis=1)
    own_f = factor[...]
    swapped = jnp.concatenate([own_f[:, half_width:], own_f[:, :half_width]], axis=1)
    own_high, own_low = split(jnp.where(feat == 0, own_f, swapped))
    all_x = jnp.concatenate(x_list + [own_x], axis=0)
    all_high = jnp.concatenate(high_list + [own_high], axis=0)
    all_low = jnp.concatenate(low_list + [own_low], axis=0)

    wide = all_x.astype(jnp.float32)
    squares = wide * wide
    norm_column = jnp.sum(squares[:total_pivots], axis=1, keepdims=True)
    square_high, square_low = split(squares)
    ones = jnp.ones((8, square_high.shape[1]), jnp.bfloat16)
    norm_row = (dot_nt(ones, square_high) + dot_nt(ones, square_low))[0:1, :]

    own_ids = half_start + lax.broadcasted_iota(jnp.int32, (1, half_rows), 1)
    id_row = jnp.concatenate([pivots[b : b + 1, :] for b in range(block_count)] + [own_ids], axis=1)
    id_column = jnp.concatenate(ids, axis=0)

    dots = dot_nt(all_x[:total_pivots], all_x)
    left = jnp.concatenate([all_high, all_high, all_low], axis=1)[:total_pivots]
    right = jnp.concatenate([all_high, all_low, all_high], axis=1)
    explained = dot_nt(left, right)
    panel = jnp.exp((2.0 * dots - norm_column - norm_row) * (1.0 / (2 * all_x.shape[1])))
    panel = panel + ridge_weight * (id_row == id_column).astype(jnp.float32)
    work[...] = panel - explained

    eliminate(work, total_pivots, total)

    removed = jnp.zeros((1, half_rows), jnp.float32)
    for block in range(block_count):
        fresh = work[block * pivot_count : (block + 1) * pivot_count, total_pivots:]
        removed = removed + jnp.sum(fresh * fresh, axis=0, keepdims=True)
        columns_out[block] = jnp.transpose(fresh)
    residual_out[...] = residual[...] - removed.reshape(half_rows)


def shards(embeddings, factor, residual_diag, pivots):
    half_rows, rank = factor.shape
    feat_cols = embeddings.shape[1]
    rows_count = lax.axis_size("rows")
    block_count, pivot_count = pivots.shape
    capacity = max(2, 2 * pivot_count // rows_count)
    slots = block_count * capacity
    stages_x = stages_of(rows_count)
    stages_f = stages_x[::-1]
    vmem = pl.BlockSpec(memory_space=pltpu.VMEM)
    limits = pltpu.CompilerParams(vmem_limit_bytes=vmem_limit)

    def cross(values):
        return lax.ppermute(values, "feat", [(0, 1), (1, 0)])

    def reach(values, offset):
        return lax.ppermute(values, "rows", [(i, i ^ offset) for i in range(rows_count)])

    def gather(held, stages):
        for stride, size in stages[:-1]:
            held = jnp.concatenate([held] + [reach(held, stride * j) for j in range(1, size)], axis=0)
        stride, size = stages[-1]
        return [held] + [reach(held, stride * j) for j in range(1, size)]

    picked_x, picked_f, other_f = pl.pallas_call(
        lambda *refs: pack_body(*refs, capacity=capacity),
        out_shape=(
            jax.ShapeDtypeStruct((slots, feat_cols), jnp.bfloat16),
            jax.ShapeDtypeStruct((slots, rank // 2), jnp.float32),
            jax.ShapeDtypeStruct((slots, rank // 2), jnp.float32),
        ),
        in_specs=[vmem, vmem, vmem],
        out_specs=(vmem, vmem, vmem),
        compiler_params=limits,
        name="pack",
    )(pivots, embeddings, factor)
    far_x = cross(embeddings)
    held_f = (picked_f + cross(other_f)).astype(jnp.float16)
    mine_x = gather(picked_x, stages_x)
    mine_f = gather(held_f, stages_f)
    theirs_x = [cross(piece) for piece in mine_x]
    theirs_f = [cross(piece) for piece in mine_f]
    mine_f = jnp.concatenate(mine_f, axis=0).astype(jnp.float32)
    theirs_f = jnp.concatenate(theirs_f, axis=0).astype(jnp.float32)

    total_pivots = block_count * pivot_count
    return pl.pallas_call(
        lambda *refs: main_body(*refs, capacity=capacity, stages_x=stages_x, stages_f=stages_f),
        out_shape=(
            jax.ShapeDtypeStruct((block_count, half_rows, pivot_count), jnp.float32),
            jax.ShapeDtypeStruct((half_rows,), jnp.float32),
        ),
        in_specs=[vmem] * (7 + 2 * len(mine_x)),
        out_specs=(vmem, vmem),
        scratch_shapes=[pltpu.VMEM((total_pivots, total_pivots + half_rows), jnp.float32)],
        compiler_params=limits,
        name="extend",
    )(pivots, embeddings, far_x, factor, residual_diag, *mine_x, *theirs_x, mine_f, theirs_f)


def solution(mesh):
    return jax.shard_map(
        shards,
        mesh=mesh,
        in_specs=(P("rows", "feat"), P(("rows", "feat"), None), P(("rows", "feat")), P()),
        out_specs=(P(None, ("rows", "feat"), None), P(("rows", "feat"))),
        check_vma=False,
    )
```
